32 devices in a mesh: req: 8 (over z, y), tp: 4 (over x, core).
Axes of the slice: x: 2, y: 2, z: 4, core: 2. Of those that a mesh axis runs over, the one named last changes fastest.
Arguments:
- tokens: bfloat16 [16384, 8192], P('req', 'tp'), may hold values from -6 to 6
- base_projection_weight: bfloat16 [8192, 2048], P('tp'), may hold values from -0.0625 to 0.0625
- adapter_down_maps: bfloat16 [128, 8192, 128], P('req', 'tp'), may hold values from -0.0625 to 0.0625
- adapter_up_maps: bfloat16 [128, 64, 2048], P('req', None, 'tp'), may hold values from -0.75 to 0.75
- block_adapter_ids: int32 [128], replicated, may hold values from 0 to 128, as said below
- adapter_storage_entry: int32 [128], replicated, may hold values from 0 to 127, as said below
Outputs:
- key_value: bfloat16 [16384, 2048], P('req', 'tp')
The draws below stay inside these ranges and needn't reach their ends.
Inputs may be any that keep to these rules, and one draw needn't show every extreme that they name: `block_adapter_ids`: ids are 0 (base model) or 1 to 128. Adapter k is held by req index adapter_storage_entry[k - 1] // 16. Among the 16 blocks of one req index (blocks i * 16 to i * 16 + 15) at most 2 name adapters held by any one req index; in every draw one req index receives exactly 2 blocks, all naming one adapter, from every req index. `adapter_storage_entry`: A permutation: each storage entry holds exactly one adapter.
All inputs are finite; a program needn't handle non-finite values.
Results may differ from the reference program's by a relative error of at most 0.014.
Values may be sent and summed in bfloat16 or wider, within the bound.
A program may use at most 128 MiB of HBM per device.

```python
import jax
import jax.numpy as jnp
from jax import lax

MODEL_WIDTH = 8192
KEY_WIDTH = 1024
ADAPTER_RANK = 64
BLOCK = 128
CAP = 2
BLK_DEV = 16
ADP_DEV = 16
ROWS = 16384
BLOCKS = 128
ADAPTER_TOTAL = 128
N_REQ = 8
N_TP = 4


def adapter_tables(key):
    folded = jax.random.fold_in(key, 31)
    key_slot, key_hot, key_local, key_perm, key_pick, key_other, key_kind, key_order = jax.random.split(folded, 8)
    slot_map = jax.random.permutation(key_slot, ADAPTER_TOTAL).astype(jnp.int32)
    inverse = jnp.zeros((ADAPTER_TOTAL,), jnp.int32).at[slot_map].set(jnp.arange(ADAPTER_TOTAL, dtype=jnp.int32))
    lane_count = BLK_DEV // CAP
    hot_owner = jax.random.randint(key_hot, (), 0, N_REQ).astype(jnp.int32)
    hot_local = jax.random.randint(key_local, (), 0, ADP_DEV).astype(jnp.int32)
    others = jax.vmap(lambda subkey: jax.random.permutation(subkey, N_REQ - 1))(jax.random.split(key_perm, N_REQ)).astype(jnp.int32)
    lane_owner = jnp.concatenate([jnp.full((N_REQ, 1), hot_owner, jnp.int32), (hot_owner + 1 + others[:, :lane_count - 1]) % N_REQ], axis=1)
    picked = jax.random.randint(key_pick, (N_REQ, lane_count), 0, ADP_DEV).astype(jnp.int32)
    lane_local = picked.at[:, 0].set(hot_local)
    first_ids = inverse[lane_owner * ADP_DEV + lane_local] + 1
    other_local = jax.random.randint(key_other, (N_REQ, lane_count), 0, ADP_DEV).astype(jnp.int32)
    other_ids = inverse[lane_owner * ADP_DEV + other_local] + 1
    second_kind = jax.random.randint(key_kind, (N_REQ, lane_count), 0, 4).astype(jnp.int32).at[:, 0].set(2)
    second = jnp.where(second_kind == 0, 0, jnp.where(second_kind == 1, other_ids, first_ids))
    paired = jnp.stack([first_ids, second], axis=2).reshape(N_REQ, lane_count * 2)
    block_order = jax.vmap(lambda subkey: jax.random.permutation(subkey, BLK_DEV))(jax.random.split(key_order, N_REQ)).astype(jnp.int32)
    blocks = jnp.take_along_axis(paired, block_order, axis=1)
    return (slot_map, blocks.reshape(N_REQ * BLK_DEV).astype(jnp.int32))


def draw_adapter_storage_entry(key, part):
    return adapter_tables(key)[0]


def draw_block_adapter_ids(key, part):
    return adapter_tables(key)[1]


def block_scale(stream_key, extent, cuts, smallest, largest):
    def one(axis_at, shards_of):
        heights = jax.random.uniform(jax.random.fold_in(jax.random.fold_in(stream_key, 6), axis_at), (shards_of,), jnp.float32, smallest / len(cuts), largest / len(cuts))
        return jnp.repeat(jnp.exp(heights), extent[axis_at] // shards_of).reshape((-1,) + (1,) * (len(extent) - axis_at - 1))

    gain = one(*cuts[0])
    for cut in cuts[1:]:
        gain = gain * one(*cut)
    return gain


def scatter_about(key, dims, deviation, limit, cuts=(), kind=jnp.bfloat16):
    values = jax.random.normal(key, dims, jnp.float32) * deviation
    if len(cuts) > 0:
        values = block_scale(key, dims, cuts, -0.22, 0.18) * values
    return jnp.clip(values, min=-limit, max=limit).astype(kind)


def setup_inputs(seed: int = 0) -> dict:
    key_list = jax.random.split(jax.random.key(seed), 7)
    return {
        "tokens": scatter_about(key_list[0], (ROWS, MODEL_WIDTH), 1.0, 6.0, ((0, 8), (1, 4))),
        "base_projection_weight": scatter_about(key_list[1], (MODEL_WIDTH, 2 * KEY_WIDTH), MODEL_WIDTH ** -0.5, 0.0625, ((0, 4),)),
        "adapter_down_maps": scatter_about(key_list[2], (ADAPTER_TOTAL, MODEL_WIDTH, 2 * ADAPTER_RANK), MODEL_WIDTH ** -0.5, 0.0625, ((0, 8), (1, 4))),
        "adapter_up_maps": scatter_about(key_list[3], (ADAPTER_TOTAL, ADAPTER_RANK, 2 * KEY_WIDTH), ADAPTER_RANK ** -0.5, 0.75, ((0, 8), (2, 4))),
        "block_adapter_ids": draw_block_adapter_ids(jax.random.fold_in(key_list[6], 71), 0),
        "adapter_storage_entry": draw_adapter_storage_entry(jax.random.fold_in(key_list[6], 71), 0),
    }


def reference(tokens, base_projection_weight, adapter_down_maps, adapter_up_maps, block_adapter_ids, adapter_storage_entry):
    group_width = MODEL_WIDTH // N_TP
    base_sum = jnp.zeros((tokens.shape[0], 2 * KEY_WIDTH), jnp.float32)
    for group_index in range(N_TP):
        offset = group_index * group_width
        product = jnp.dot(tokens[:, offset:offset + group_width], base_projection_weight[offset:offset + group_width], preferred_element_type=jnp.float32).astype(jnp.bfloat16)
        base_sum = base_sum + lax.optimization_barrier(product).astype(jnp.float32)
    entries = adapter_storage_entry[jnp.maximum(block_adapter_ids - 1, 0)].astype(jnp.int32)
    blocks = tokens.reshape(BLOCKS, BLOCK, MODEL_WIDTH)

    def one_block(inputs):
        block_rows, storage_index, adapter_id = inputs
        down_projected = jnp.dot(block_rows, adapter_down_maps[storage_index], preferred_element_type=jnp.float32).astype(jnp.bfloat16)
        up_weight_matrix = adapter_up_maps[storage_index]
        key_part = jnp.dot(down_projected[:, :ADAPTER_RANK], up_weight_matrix[:, :KEY_WIDTH], preferred_element_type=jnp.float32)
        value_part = jnp.dot(down_projected[:, ADAPTER_RANK:], up_weight_matrix[:, KEY_WIDTH:], preferred_element_type=jnp.float32)
        block_delta = jnp.concatenate([key_part, value_part], axis=1).astype(jnp.bfloat16)
        return jnp.where(adapter_id > 0, block_delta, jnp.zeros_like(block_delta))

    deltas = lax.map(one_block, (blocks, entries, block_adapter_ids))
    deltas = lax.optimization_barrier(deltas).reshape(BLOCKS * BLOCK, 2 * KEY_WIDTH).astype(jnp.float32)
    return (base_sum + deltas).astype(jnp.bfloat16)
```

```python
import functools

import jax
import jax.numpy as jnp
from jax import lax
from jax.experimental import pallas as pl
from jax.experimental.pallas import tpu as pltpu
from jax.sharding import PartitionSpec as P

KEY_WIDTH = 1024
BLOCK = 128
CAP = 2


def shrink_body(blk_ref, tok_a, tok_b, down_a, down_b, out_ref):
    rank = out_ref.shape[-1] // 2
    one = jnp.dot(tok_a[...], down_a[0], preferred_element_type=jnp.float32).astype(out_ref.dtype)
    two = jnp.dot(tok_b[...], down_b[0], preferred_element_type=jnp.float32).astype(out_ref.dtype)
    out_ref[0, 0] = jnp.concatenate([one[:, :rank], two[:, :rank]], axis=1)
    out_ref[1, 0] = jnp.concatenate([one[:, rank:], two[:, rank:]], axis=1)


def shrink_pairs(tokens, downs, blk_of):
    items, feat, width = downs.shape
    pairs = items // 2
    return pl.pallas_call(
        shrink_body,
        grid_spec=pltpu.PrefetchScalarGridSpec(
            num_scalar_prefetch=1,
            grid=(pairs,),
            in_specs=[
                pl.BlockSpec((BLOCK, feat), lambda p, blk: (blk[2 * p], 0)),
                pl.BlockSpec((BLOCK, feat), lambda p, blk: (blk[2 * p + 1], 0)),
                pl.BlockSpec((1, feat, width), lambda p, blk: (2 * p, 0, 0)),
                pl.BlockSpec((1, feat, width), lambda p, blk: (2 * p + 1, 0, 0)),
            ],
            out_specs=pl.BlockSpec((2, 1, BLOCK, width), lambda p, blk: (0, p, 0, 0)),
        ),
        out_shape=jax.ShapeDtypeStruct((2, pairs, BLOCK, width), tokens.dtype),
        cost_estimate=pl.CostEstimate(
            flops=2 * items * BLOCK * feat * width,
            bytes_accessed=2 * items * feat * (BLOCK + width),
            transcendentals=0,
        ),
    )(blk_of, tokens, tokens, downs, downs)


def finish_body(spot_ref, live_ref, base_ref, shrink_ref, up_ref, out_ref):
    b = pl.program_id(0)
    rank = up_ref.shape[1]
    odd = spot_ref[b] % 2
    both = shrink_ref[0]
    mine = jnp.where(odd == 1, both[:, rank:], both[:, :rank])
    delta = jnp.dot(mine, up_ref[0], preferred_element_type=jnp.float32)
    delta = delta.astype(jnp.bfloat16).astype(jnp.float32)
    delta = jnp.where(live_ref[b] > 0, delta, jnp.zeros_like(delta))
    out_ref[...] = (base_ref[...].astype(jnp.float32) + delta).astype(out_ref.dtype)


def finish(base, shrunk, ups, spot, live):
    rows, cols = base.shape
    rank = ups.shape[1]
    return pl.pallas_call(
        finish_body,
        grid_spec=pltpu.PrefetchScalarGridSpec(
            num_scalar_prefetch=2,
            grid=(rows // BLOCK,),
            in_specs=[
                pl.BlockSpec((BLOCK, cols), lambda b, spot, live: (b, 0)),
                pl.BlockSpec((1, BLOCK, 2 * rank), lambda b, spot, live: (spot[b] // 2, 0, 0)),
                pl.BlockSpec((1, rank, cols), lambda b, spot, live: (spot[b], 0, 0)),
            ],
            out_specs=pl.BlockSpec((BLOCK, cols), lambda b, spot, live: (b, 0)),
        ),
        out_shape=jax.ShapeDtypeStruct((rows, cols), base.dtype),
    )(spot, live, base, shrunk, ups)


def per_device(
    tokens,
    base_projection_weight,
    adapter_down_maps,
    adapter_up_maps,
    block_adapter_ids,
    adapter_storage_entry,
):
    req_count = lax.axis_size("req")
    tp_count = lax.axis_size("tp")
    my_req = lax.axis_index("req")
    row_count, feat_count = tokens.shape
    blk_count = row_count // BLOCK
    adapter_count = adapter_down_maps.shape[0]

    ids_all = block_adapter_ids.reshape(req_count, blk_count)
    stored = adapter_storage_entry[jnp.maximum(ids_all - 1, 0)]
    owner_all = jnp.where(ids_all > 0, stored // adapter_count, -1)
    local_all = stored % adapter_count
    block_pos = jnp.arange(blk_count, dtype=jnp.int32)
    before = block_pos[None, :] < block_pos[:, None]
    same_owner = owner_all[:, :, None] == owner_all[:, None, :]
    slot_all = jnp.sum(same_owner & before[None], axis=2)
    slot_ids = jnp.arange(CAP, dtype=jnp.int32)[:, None, None]
    incoming = (owner_all[None] == my_req) & (slot_all[None] == slot_ids)
    send_local = jnp.sum(jnp.where(incoming, local_all[None], 0), axis=2)
    ids_own = lax.dynamic_index_in_dim(ids_all, my_req, 0, keepdims=False)
    owner_own = lax.dynamic_index_in_dim(owner_all, my_req, 0, keepdims=False)
    slot_own = lax.dynamic_index_in_dim(slot_all, my_req, 0, keepdims=False)
    owner_ids = jnp.arange(req_count, dtype=jnp.int32)[None, :, None]
    outgoing = (owner_own[None, None] == owner_ids) & (slot_own[None, None] == slot_ids)
    blk_of = jnp.sum(jnp.where(outgoing, block_pos[None, None], 0), axis=2)
    live = (ids_own > 0).astype(jnp.int32)
    spot = jnp.where(ids_own > 0, slot_own * req_count + owner_own, 0)

    swap = functools.partial(lax.all_to_all, axis_name="req", split_axis=0, concat_axis=0, tiled=True)
    downs = [swap(adapter_down_maps[send_local[s]]) for s in range(CAP)]
    ups = [swap(adapter_up_maps[send_local[s]]) for s in range(CAP)]

    partial_value = jnp.dot(tokens, base_projection_weight, preferred_element_type=jnp.float32)
    partial_value, blk_of = lax.optimization_barrier((partial_value.astype(jnp.bfloat16), blk_of))
    base = lax.psum_scatter(
        partial_value, "tp", scatter_dimension=1, tiled=True
    )

    split = tp_count // 2
    groups = [list(range(split)), list(range(split, tp_count))]
    shrunk = []
    for s in range(CAP):
        part = shrink_pairs(tokens, downs[s], blk_of[s])
        part = part.reshape((tp_count, part.shape[1] // split) + part.shape[2:])
        mine = lax.psum_scatter(part, "tp", scatter_dimension=0, tiled=False)
        shrunk.append(lax.all_gather(mine, "tp", axis_index_groups=groups, axis=0, tiled=True))
    return finish(base, jnp.concatenate(shrunk), jnp.concatenate(ups), spot, live)


def solution(mesh):
    placed = (P("req", "tp"), P("tp", None), P("req", "tp", None), P("req", None, "tp"), P(), P())
    return jax.shard_map(
        per_device, mesh=mesh, in_specs=placed, out_specs=P("req", "tp"), check_vma=False
    )
```

```python
import functools

import jax
import jax.numpy as jnp
from jax import lax
from jax.experimental import pallas as pl
from jax.experimental.pallas import tpu as pltpu
from jax.sharding import PartitionSpec as P

KEY_WIDTH = 1024
BLOCK = 128
CAP = 2
LANES = 128
MESH = pl.DeviceIdType.MESH


def pack_body(idx_ref, down_ref, up_ref, out_ref):
    feat = down_ref.shape[1]
    rank = up_ref.shape[1]
    out_ref[0, :feat] = down_ref[0]
    for c in range(up_ref.shape[2] // LANES):
        out_ref[0, feat + c * rank:feat + (c + 1) * rank] = up_ref[0, :, c * LANES:(c + 1) * LANES]


def pack(downs, ups, idx):
    count = idx.shape[0]
    feat, width = downs.shape[1:]
    rank, cols = ups.shape[1:]
    rows = feat + rank * cols // LANES
    return pl.pallas_call(
        pack_body,
        grid_spec=pltpu.PrefetchScalarGridSpec(
            num_scalar_prefetch=1,
            grid=(count,),
            in_specs=[
                pl.BlockSpec((1, feat, width), lambda p, idx: (idx[p], 0, 0)),
                pl.BlockSpec((1, rank, cols), lambda p, idx: (idx[p], 0, 0)),
            ],
            out_specs=pl.BlockSpec((1, rows, width), lambda p, idx: (p, 0, 0)),
        ),
        out_shape=jax.ShapeDtypeStruct((count, rows, width), downs.dtype),
        cost_estimate=pl.CostEstimate(
            flops=0, bytes_accessed=4 * count * rows * width, transcendentals=0
        ),
    )(idx, downs, ups)


def shrink_body(blk_ref, tok_a, tok_b, down_a, down_b, out_ref):
    rank = out_ref.shape[-1] // 2
    one = jnp.dot(tok_a[...], down_a[0], preferred_element_type=jnp.float32).astype(out_ref.dtype)
    two = jnp.dot(tok_b[...], down_b[0], preferred_element_type=jnp.float32).astype(out_ref.dtype)
    out_ref[0, 0] = jnp.concatenate([one[:, :rank], two[:, :rank]], axis=1)
    out_ref[1, 0] = jnp.concatenate([one[:, rank:], two[:, rank:]], axis=1)


def shrink_pairs(tokens, packed, blk_of):
    items, _, width = packed.shape
    feat = tokens.shape[1]
    pairs = items // 2
    return pl.pallas_call(
        shrink_body,
        grid_spec=pltpu.PrefetchScalarGridSpec(
            num_scalar_prefetch=1,
            grid=(pairs,),
            in_specs=[
                pl.BlockSpec((BLOCK, feat), lambda p, blk: (blk[2 * p], 0)),
                pl.BlockSpec((BLOCK, feat), lambda p, blk: (blk[2 * p + 1], 0)),
                pl.BlockSpec((1, feat, width), lambda p, blk: (2 * p, 0, 0)),
                pl.BlockSpec((1, feat, width), lambda p, blk: (2 * p + 1, 0, 0)),
            ],
            out_specs=pl.BlockSpec((2, 1, BLOCK, width), lambda p, blk: (0, p, 0, 0)),
        ),
        out_shape=jax.ShapeDtypeStruct((2, pairs, BLOCK, width), tokens.dtype),
        cost_estimate=pl.CostEstimate(
            flops=2 * items * BLOCK * feat * width,
            bytes_accessed=2 * items * feat * (BLOCK + width),
            transcendentals=0,
        ),
    )(blk_of, tokens, tokens, packed, packed)


def exchange_body(n, part_ref, out_ref, landed, send_sem, recv_sem):
    me = lax.axis_index("tp")
    barrier = pltpu.get_barrier_semaphore()
    for d in range(1, n):
        pl.semaphore_signal(
            barrier, inc=1, device_id={"tp": lax.rem(me + d, n)}, device_id_type=MESH
        )
    pl.semaphore_wait(barrier, n - 1)
    copies = []
    for d in range(1, n):
        to = lax.rem(me + d, n)
        copy = pltpu.make_async_remote_copy(
            src_ref=part_ref.at[to // (n // 2)],
            dst_ref=landed.at[d - 1],
            send_sem=send_sem.at[d - 1],
            recv_sem=recv_sem.at[d - 1],
            device_id={"tp": to},
            device_id_type=MESH,
        )
        copy.start()
        copies.append(copy)
    for copy in copies:
        copy.wait()
    total = part_ref[me // (n // 2)].astype(jnp.float32)
    for d in range(1, n):
        total = total + landed[d - 1].astype(jnp.float32)
    out_ref[...] = total.astype(out_ref.dtype)


def exchange(part, n, collective_id):
    shape = part.shape[1:]
    return pl.pallas_call(
        functools.partial(exchange_body, n),
        out_shape=jax.ShapeDtypeStruct(shape, part.dtype),
        in_specs=[pl.BlockSpec(memory_space=pltpu.VMEM)],
        out_specs=pl.BlockSpec(memory_space=pltpu.VMEM),
        scratch_shapes=[
            pltpu.VMEM((n - 1,) + shape, part.dtype),
            pltpu.SemaphoreType.DMA((n - 1,)),
            pltpu.SemaphoreType.DMA((n - 1,)),
        ],
        compiler_params=pltpu.CompilerParams(collective_id=collective_id, has_side_effects=True),
    )(part)


def finish_body(req_count, per_step, spot_ref, live_ref, base_ref, s0, s1, u0, u1, out_ref):
    rank = s0.shape[-1] // 2
    for k in range(per_step):
        b = pl.program_id(0) * per_step + k
        spot = spot_ref[b]
        second = spot // req_count == 1
        owner = lax.rem(spot, req_count)
        both = jnp.where(second, s1[owner // 2], s0[owner // 2])
        mine = jnp.where(lax.rem(owner, 2) == 1, both[:, rank:], both[:, :rank])
        up = jnp.where(second, u1[owner], u0[owner])
        rows = slice(k * BLOCK, (k + 1) * BLOCK)
        for c in range(out_ref.shape[1] // LANES):
            delta = jnp.dot(
                mine, up[c * rank:(c + 1) * rank], preferred_element_type=jnp.float32
            )
            delta = delta.astype(jnp.bfloat16).astype(jnp.float32)
            delta = jnp.where(live_ref[b] > 0, delta, jnp.zeros_like(delta))
            cols = slice(c * LANES, (c + 1) * LANES)
            out_ref[rows, cols] = (base_ref[rows, cols].astype(jnp.float32) + delta).astype(
                out_ref.dtype
            )


def finish(base, shrunk, packed, spot, live):
    rows, cols = base.shape
    items, total_rows, width = packed[0].shape
    rank = width // 2
    up_rows = rank * cols // LANES
    per_step = 4
    whole = pl.BlockSpec(shrunk[0].shape, lambda g, spot, live: (0, 0, 0))
    ups = pl.BlockSpec(
        (items, up_rows, width), lambda g, spot, live: (0, total_rows // up_rows - 1, 0)
    )
    mine = pl.BlockSpec((per_step * BLOCK, cols), lambda g, spot, live: (g, 0))
    return pl.pallas_call(
        functools.partial(finish_body, items, per_step),
        grid_spec=pltpu.PrefetchScalarGridSpec(
            num_scalar_prefetch=2,
            grid=(rows // (per_step * BLOCK),),
            in_specs=[mine, whole, whole, ups, ups],
            out_specs=mine,
        ),
        out_shape=jax.ShapeDtypeStruct((rows, cols), base.dtype),
    )(spot, live, base, shrunk[0], shrunk[1], packed[0], packed[1])


def per_device(
    tokens,
    base_projection_weight,
    adapter_down_maps,
    adapter_up_maps,
    block_adapter_ids,
    adapter_storage_entry,
):
    req_count = lax.axis_size("req")
    tp_count = lax.axis_size("tp")
    my_req = lax.axis_index("req")
    row_count, feat_count = tokens.shape
    blk_count = row_count // BLOCK
    adapter_count = adapter_down_maps.shape[0]

    ids_all = block_adapter_ids.reshape(req_count, blk_count)
    stored = adapter_storage_entry[jnp.maximum(ids_all - 1, 0)]
    owner_all = jnp.where(ids_all > 0, stored // adapter_count, -1)
    local_all = stored % adapter_count
    block_pos = jnp.arange(blk_count, dtype=jnp.int32)
    before = block_pos[None, :] < block_pos[:, None]
    same_owner = owner_all[:, :, None] == owner_all[:, None, :]
    slot_all = jnp.sum(same_owner & before[None], axis=2)
    slot_ids = jnp.arange(CAP, dtype=jnp.int32)[:, None, None]
    incoming = (owner_all[None] == my_req) & (slot_all[None] == slot_ids)
    send_local = jnp.sum(jnp.where(incoming, local_all[None], 0), axis=2)
    ids_own = lax.dynamic_index_in_dim(ids_all, my_req, 0, keepdims=False)
    owner_own = lax.dynamic_index_in_dim(owner_all, my_req, 0, keepdims=False)
    slot_own = lax.dynamic_index_in_dim(slot_all, my_req, 0, keepdims=False)
    owner_ids = jnp.arange(req_count, dtype=jnp.int32)[None, :, None]
    outgoing = (owner_own[None, None] == owner_ids) & (slot_own[None, None] == slot_ids)
    blk_of = jnp.sum(jnp.where(outgoing, block_pos[None, None], 0), axis=2)
    live = (ids_own > 0).astype(jnp.int32)
    spot = jnp.where(ids_own > 0, slot_own * req_count + owner_own, 0)

    swap = functools.partial(lax.all_to_all, axis_name="req", split_axis=0, concat_axis=0, tiled=True)
    sent = pack(adapter_down_maps, adapter_up_maps, send_local[0])
    sent, later = lax.optimization_barrier((sent, send_local[1]))
    first = swap(sent)
    sent_later = pack(adapter_down_maps, adapter_up_maps, later)
    sent_later, weight = lax.optimization_barrier((sent_later, base_projection_weight))
    second = swap(sent_later)
    partial_value = jnp.dot(tokens, weight, preferred_element_type=jnp.float32)
    partial_value = partial_value.astype(jnp.bfloat16)
    first, partial_value = lax.optimization_barrier((first, partial_value))
    base = lax.psum_scatter(partial_value, "tp", scatter_dimension=1, tiled=True)

    packed = [first, second]
    shrunk = [
        exchange(shrink_pairs(tokens, packed[s], blk_of[s]), tp_count, s) for s in range(CAP)
    ]
    return finish(base, shrunk, packed, spot, live)


def solution(mesh):
    placed = (P("req", "tp"), P("tp", None), P("req", "tp", None), P("req", None, "tp"), P(), P())
    return jax.shard_map(
        per_device, mesh=mesh, in_specs=placed, out_specs=P("req", "tp"), check_vma=False
    )
```

```python
import functools

import jax
import jax.numpy as jnp
from jax import lax
from jax.experimental import pallas as pl
from jax.experimental.pallas import tpu as pltpu
from jax.sharding import PartitionSpec as P

KEY_WIDTH = 1024
BLOCK = 128
CAP = 2
LANES = 128
MESH = pl.DeviceIdType.MESH


def pack_body(idx_ref, down_ref, up_ref, out_ref, sem):
    feat = down_ref.shape[1]
    rank, cols = up_ref.shape[1:]
    copies = []
    for p in range(out_ref.shape[0]):
        entry = idx_ref[p]
        copies.append(
            pltpu.make_async_copy(down_ref.at[entry], out_ref.at[p, pl.ds(0, feat)], sem.at[p, 0])
        )
        for c in range(cols // LANES):
            copies.append(
                pltpu.make_async_copy(
                    up_ref.at[entry, :, pl.ds(c * LANES, LANES)],
                    out_ref.at[p, pl.ds(feat + c * rank, rank)],
                    sem.at[p, 1 + c],
                )
            )
    for copy in copies:
        copy.start()
    for copy in copies:
        copy.wait()


def pack(downs, ups, idx):
    count = idx.shape[0]
    feat, width = downs.shape[1:]
    rank, cols = ups.shape[1:]
    rows = feat + rank * cols // LANES
    return pl.pallas_call(
        pack_body,
        grid_spec=pltpu.PrefetchScalarGridSpec(
            num_scalar_prefetch=1,
            grid=(1,),
            in_specs=[pl.BlockSpec(memory_space=pl.ANY)] * 2,
            out_specs=pl.BlockSpec(memory_space=pl.ANY),
            scratch_shapes=[pltpu.SemaphoreType.DMA((count, 1 + cols // LANES))],
        ),
        out_shape=jax.ShapeDtypeStruct((count, rows, width), downs.dtype),
        cost_estimate=pl.CostEstimate(
            flops=0, bytes_accessed=4 * count * rows * width, transcendentals=0
        ),
    )(idx, downs, ups)


def shrink_body(n, tok_ref, down_ref, out_ref, part, landed, send_sem, recv_sem):
    p = pl.program_id(0)
    pairs = part.shape[1]
    rank = out_ref.shape[-1] // 2
    me = lax.axis_index("tp")
    barrier = pltpu.get_barrier_semaphore()

    @pl.when(p == 0)
    def _():
        for d in range(1, n):
            pl.semaphore_signal(
                barrier, inc=1, device_id={"tp": lax.rem(me + d, n)}, device_id_type=MESH
            )
        pl.semaphore_wait(barrier, n - 1)

    one = jnp.dot(tok_ref[0], down_ref[0], preferred_element_type=jnp.float32).astype(part.dtype)
    two = jnp.dot(tok_ref[1], down_ref[1], preferred_element_type=jnp.float32).astype(part.dtype)
    part[0, p] = jnp.concatenate([one[:, :rank], two[:, :rank]], axis=1)
    part[1, p] = jnp.concatenate([one[:, rank:], two[:, rank:]], axis=1)

    def copy_of(d, pair):
        to = lax.rem(me + d, n)
        return pltpu.make_async_remote_copy(
            src_ref=part.at[to // (n // 2), pair],
            dst_ref=landed.at[d - 1, pair],
            send_sem=send_sem.at[d - 1, pair],
            recv_sem=recv_sem.at[d - 1, pair],
            device_id={"tp": to},
            device_id_type=MESH,
        )

    for d in range(1, n):
        copy_of(d, p).start()

    @pl.when(p == pairs - 1)
    def _():
        for pair in range(pairs):
            for d in range(1, n):
                copy_of(d, pair).wait()
            total = part[me // (n // 2), pair].astype(jnp.float32)
            for d in range(1, n):
                total = total + landed[d - 1, pair].astype(jnp.float32)
            out_ref[pair] = total.astype(out_ref.dtype)


def shrink(tok_blocks, packed, slot, n):
    items, _, width = packed.shape
    feat = tok_blocks.shape[2]
    pairs = items // 2
    shape = (pairs, BLOCK, width)
    return pl.pallas_call(
        functools.partial(shrink_body, n),
        grid=(pairs,),
        in_specs=[
            pl.BlockSpec((2, BLOCK, feat), lambda p: (slot * pairs + p, 0, 0)),
            pl.BlockSpec((2, feat, width), lambda p: (p, 0, 0)),
        ],
        out_specs=pl.BlockSpec(shape, lambda p: (0, 0, 0)),
        out_shape=jax.ShapeDtypeStruct(shape, packed.dtype),
        scratch_shapes=[
            pltpu.VMEM((2,) + shape, packed.dtype),
            pltpu.VMEM((n - 1,) + shape, packed.dtype),
            pltpu.SemaphoreType.DMA((n - 1, pairs)),
            pltpu.SemaphoreType.DMA((n - 1, pairs)),
        ],
        compiler_params=pltpu.CompilerParams(collective_id=slot, has_side_effects=True),
        cost_estimate=pl.CostEstimate(
            flops=2 * items * BLOCK * feat * width,
            bytes_accessed=2 * items * feat * (BLOCK + width),
            transcendentals=0,
        ),
    )(tok_blocks, packed)


def finish_body(req_count, per_step, spot_ref, live_ref, base_ref, s0, s1, u0, u1, out_ref):
    rank = s0.shape[-1] // 2
    for k in range(per_step):
        b = pl.program_id(0) * per_step + k
        spot = spot_ref[b]
        second = spot // req_count == 1
        owner = lax.rem(spot, req_count)
        both = jnp.where(second, s1[owner // 2], s0[owner // 2])
        mine = jnp.where(lax.rem(owner, 2) == 1, both[:, rank:], both[:, :rank])
        up = jnp.where(second, u1[owner], u0[owner])
        rows = slice(k * BLOCK, (k + 1) * BLOCK)
        for c in range(out_ref.shape[1] // LANES):
            delta = jnp.dot(
                mine, up[c * rank:(c + 1) * rank], preferred_element_type=jnp.float32
            )
            delta = delta.astype(jnp.bfloat16).astype(jnp.float32)
            delta = jnp.where(live_ref[b] > 0, delta, jnp.zeros_like(delta))
            cols = slice(c * LANES, (c + 1) * LANES)
            out_ref[rows, cols] = (base_ref[rows, cols].astype(jnp.float32) + delta).astype(
                out_ref.dtype
            )


def finish(base, shrunk, packed, spot, live):
    rows, cols = base.shape
    items, total_rows, width = packed[0].shape
    rank = width // 2
    up_rows = rank * cols // LANES
    per_step = 4
    whole = pl.BlockSpec(shrunk[0].shape, lambda g, spot, live: (0, 0, 0))
    ups = pl.BlockSpec(
        (items, up_rows, width), lambda g, spot, live: (0, total_rows // up_rows - 1, 0)
    )
    mine = pl.BlockSpec((per_step * BLOCK, cols), lambda g, spot, live: (g, 0))
    return pl.pallas_call(
        functools.partial(finish_body, items, per_step),
        grid_spec=pltpu.PrefetchScalarGridSpec(
            num_scalar_prefetch=2,
            grid=(rows // (per_step * BLOCK),),
            in_specs=[mine, whole, whole, ups, ups],
            out_specs=mine,
        ),
        out_shape=jax.ShapeDtypeStruct((rows, cols), base.dtype),
    )(spot, live, base, shrunk[0], shrunk[1], packed[0], packed[1])


def per_device(
    tokens,
    base_projection_weight,
    adapter_down_maps,
    adapter_up_maps,
    block_adapter_ids,
    adapter_storage_entry,
):
    req_count = lax.axis_size("req")
    tp_count = lax.axis_size("tp")
    my_req = lax.axis_index("req")
    row_count, feat_count = tokens.shape
    blk_count = row_count // BLOCK
    adapter_count = adapter_down_maps.shape[0]

    ids_all = block_adapter_ids.reshape(req_count, blk_count)
    stored = adapter_storage_entry[jnp.maximum(ids_all - 1, 0)]
    owner_all = jnp.where(ids_all > 0, stored // adapter_count, -1)
    local_all = stored % adapter_count
    block_pos = jnp.arange(blk_count, dtype=jnp.int32)
    before = block_pos[None, :] < block_pos[:, None]
    same_owner = owner_all[:, :, None] == owner_all[:, None, :]
    slot_all = jnp.sum(same_owner & before[None], axis=2)
    slot_ids = jnp.arange(CAP, dtype=jnp.int32)[:, None, None]
    incoming = (owner_all[None] == my_req) & (slot_all[None] == slot_ids)
    send_local = jnp.sum(jnp.where(incoming, local_all[None], 0), axis=2)
    ids_own = lax.dynamic_index_in_dim(ids_all, my_req, 0, keepdims=False)
    owner_own = lax.dynamic_index_in_dim(owner_all, my_req, 0, keepdims=False)
    slot_own = lax.dynamic_index_in_dim(slot_all, my_req, 0, keepdims=False)
    owner_ids = jnp.arange(req_count, dtype=jnp.int32)[None, :, None]
    outgoing = (owner_own[None, None] == owner_ids) & (slot_own[None, None] == slot_ids)
    blk_of = jnp.sum(jnp.where(outgoing, block_pos[None, None], 0), axis=2)
    live = (ids_own > 0).astype(jnp.int32)
    spot = jnp.where(ids_own > 0, slot_own * req_count + owner_own, 0)

    swap = functools.partial(lax.all_to_all, axis_name="req", split_axis=0, concat_axis=0, tiled=True)
    sent = pack(adapter_down_maps, adapter_up_maps, send_local[0])
    sent, later = lax.optimization_barrier((sent, send_local[1]))
    first = swap(sent)
    sent_later = pack(adapter_down_maps, adapter_up_maps, later)
    sent_later, weight, picked = lax.optimization_barrier(
        (sent_later, base_projection_weight, blk_of.reshape(-1))
    )
    second = swap(sent_later)
    partial_value = jnp.dot(tokens, weight, preferred_element_type=jnp.float32)
    partial_value = partial_value.astype(jnp.bfloat16)
    tok_blocks = tokens.reshape(blk_count, BLOCK, feat_count)[picked]
    first, partial_value, tok_blocks = lax.optimization_barrier((first, partial_value, tok_blocks))
    base = lax.psum_scatter(partial_value, "tp", scatter_dimension=1, tiled=True)

    packed = [first, second]
    shrunk = [shrink(tok_blocks, packed[s], s, tp_count) for s in range(CAP)]
    return finish(base, shrunk, packed, spot, live)


def solution(mesh):
    placed = (P("req", "tp"), P("tp", None), P("req", "tp", None), P("req", None, "tp"), P(), P())
    return jax.shard_map(
        per_device, mesh=mesh, in_specs=placed, out_specs=P("req", "tp"), check_vma=False
    )
```
